32 devices in a mesh: energy: 16 (over z, y, x), space: 2 (over core).
Axes of the slice: x: 2, y: 2, z: 4, core: 2. Of those that a mesh axis runs over, the one named last changes fastest.
Arguments:
- lesser: bfloat16 [32, 2, 2, 256, 256], P('energy', 'space'), may hold values from -6 to 6
- greater: bfloat16 [32, 2, 2, 256, 256], P('energy', 'space'), may hold values from -6 to 6
- coulomb_diag: bfloat16 [2, 256, 256], P('space'), may hold values from -0.375 to 0.375
- coulomb_upper: bfloat16 [2, 256, 256], P('space'), may hold values from -0.375 to 0.375
Outputs:
- screened: bfloat16 [32, 2, 2, 256, 256], P('energy', 'space')
The draws below stay inside these ranges and needn't reach their ends.
All inputs are finite; a program needn't handle non-finite values.
Results may differ from the reference program's by a relative error of at most 0.015.
Values may be sent and summed in bfloat16 or wider, within the bound.
A program may use at most 64 MiB of HBM per device.

```python
import jax
import jax.numpy as jnp
from jax import lax

BS = 256
NE = 32
NB = 2


def shard_levels(stream_key, extent, shards, low, largest):
    def one(axis_at, shards_of):
        heights = jax.random.uniform(jax.random.fold_in(jax.random.fold_in(stream_key, 6), axis_at), (shards_of,), jnp.float32, low / len(shards), largest / len(shards))
        return jnp.repeat(jnp.exp(heights), extent[axis_at] // shards_of).reshape((-1,) + (1,) * (len(extent) - axis_at - 1))

    level = one(*shards[0])
    for cut in shards[1:]:
        level = level * one(*cut)
    return level


def normal_values(rng, shape, scale, limit, cuts=(), dtype=jnp.bfloat16):
    entries = scale * jax.random.normal(rng, shape, jnp.float32)
    if cuts:
        entries = entries * shard_levels(rng, shape, cuts, -0.22, 0.18)
    return jnp.clip(entries, -limit, limit).astype(dtype)


def setup_inputs(seed: int = 0) -> dict:
    arg_keys = jax.random.split(jax.random.key(seed), 5)
    return {
        "lesser": normal_values(arg_keys[0], (NE, NB, 2, BS, BS), 1.0, 6.0, ((0, 16), (1, 2))),
        "greater": normal_values(arg_keys[1], (NE, NB, 2, BS, BS), 1.0, 6.0, ((0, 16), (1, 2))),
        "coulomb_diag": normal_values(arg_keys[2], (NB, BS, BS), BS ** -0.5, 0.375, ((0, 2),)),
        "coulomb_upper": normal_values(arg_keys[3], (NB, BS, BS), BS ** -0.5, 0.375, ((0, 2),)),
    }


def widen(values):
    return values.astype(jnp.float32)


def polar_row(lesser_row, greater_row):
    length = 2 * NE
    lesser_re = widen(lesser_row[:, 0])
    lesser_im = widen(lesser_row[:, 1])
    greater_re = widen(greater_row[:, 0])
    greater_im = widen(greater_row[:, 1])

    def forward(values):
        return jnp.fft.rfft(values, n=length, axis=0)

    def reverse(values):
        return jnp.fft.rfft(values[::-1], n=length, axis=0)

    def inverse(values):
        return jnp.fft.irfft(values, n=length, axis=0)[NE - 1:2 * NE - 1]

    spec_lre = forward(lesser_re)
    spec_lim = forward(lesser_im)
    spec_gre = reverse(greater_re)
    spec_gim = reverse(greater_im)
    corr_re = inverse(spec_lre * spec_gre - spec_lim * spec_gim).astype(jnp.float32)
    corr_im = inverse(spec_lre * spec_gim + spec_lim * spec_gre).astype(jnp.float32)
    factor = jnp.float32(NE) ** -0.5
    return jnp.stack([corr_im * factor, -corr_re * factor], axis=1).astype(jnp.bfloat16)


def reference(lesser, greater, coulomb_diag, coulomb_upper):
    greater_t = jnp.swapaxes(greater, 3, 4)

    def one_row(pair):
        return polar_row(pair[0], pair[1])

    polar = lax.map(one_row, (jnp.moveaxis(lesser, 1, 0), jnp.moveaxis(greater_t, 1, 0)))
    polar = jnp.moveaxis(polar, 0, 1)
    zero_row = jnp.zeros_like(polar[:, :1])
    polar_next = jnp.concatenate([polar[:, 1:], zero_row], axis=1)
    polar_prev = jnp.concatenate([zero_row, polar[:, :-1]], axis=1)
    upper_prev = jnp.concatenate([jnp.zeros_like(coulomb_upper[:1]), coulomb_upper[:-1]], axis=0)

    def screen(blocks):
        own, after, before = blocks
        left = jnp.einsum('iab,icbd->icad', widen(coulomb_diag), widen(own)).astype(jnp.bfloat16)
        total = jnp.einsum('icad,ifd->icaf', widen(left), widen(coulomb_diag))
        left = jnp.einsum('iab,icbd->icad', widen(coulomb_upper), widen(after)).astype(jnp.bfloat16)
        total = total + jnp.einsum('icad,ifd->icaf', widen(left), widen(coulomb_upper))
        left = jnp.einsum('iba,icbd->icad', widen(upper_prev), widen(before)).astype(jnp.bfloat16)
        total = total + jnp.einsum('icad,idf->icaf', widen(left), widen(upper_prev))
        return total.astype(jnp.bfloat16)

    return lax.map(screen, (polar, polar_next, polar_prev))
```

```python
import functools
import math

import jax
import jax.numpy as jnp
from jax import lax
from jax.experimental import pallas as pl
from jax.experimental.pallas import tpu as pltpu
from jax.sharding import PartitionSpec as P


def from_behind(value, axis, steps):
    count = lax.axis_size(axis)
    leading, last = (max(0, -steps), min(count, count - steps))
    return lax.ppermute(value, axis, [(source, source + steps) for source in range(leading, last)])


def split_parts(values):
    high = values.astype(jnp.bfloat16)
    low = (values - high.astype(jnp.float32)).astype(jnp.bfloat16)
    return (high, low)


def product_two(table, data_bf):
    return jnp.dot(table[0], data_bf, preferred_element_type=jnp.float32) + jnp.dot(
        table[1], data_bf, preferred_element_type=jnp.float32
    )


def product_three(table, data_f32):
    data_high, data_low = split_parts(data_f32)
    total = jnp.dot(table[0], data_high, preferred_element_type=jnp.float32)
    total = total + jnp.dot(table[1], data_high, preferred_element_type=jnp.float32)
    return total + jnp.dot(table[0], data_low, preferred_element_type=jnp.float32)


def correlate(lesser_x, greater_x):
    energies = lesser_x.shape[0]
    length = 2 * energies
    tail_shape = lesser_x.shape[1:]

    def flatten(values, part):
        return values[:, :, part].reshape(energies, -1)

    lesser_re = flatten(lesser_x, 0)
    lesser_im = flatten(lesser_x, 1)
    greater_re = flatten(greater_x, 0)
    greater_im = flatten(greater_x, 1)
    freqs = lax.broadcasted_iota(jnp.int32, (length, energies), 0)
    places = lax.broadcasted_iota(jnp.int32, (length, energies), 1)
    angles = 2.0 * math.pi / length * jnp.mod(freqs * places, length).astype(jnp.float32)
    cosine = split_parts(jnp.cos(angles))
    sine = split_parts(jnp.sin(angles))
    cosine_t = split_parts(jnp.cos(angles).T)
    sine_t = split_parts(jnp.sin(angles).T)
    hat_lre = product_two(cosine, lesser_re) + product_two(sine, lesser_im)
    hat_lim = product_two(cosine, lesser_im) - product_two(sine, lesser_re)
    hat_gre = product_two(cosine, greater_re) - product_two(sine, greater_im)
    hat_gim = product_two(cosine, greater_im) + product_two(sine, greater_re)
    prod_re = hat_lre * hat_gre - hat_lim * hat_gim
    prod_im = hat_lre * hat_gim + hat_lim * hat_gre
    corr_re = (product_three(cosine_t, prod_re) - product_three(sine_t, prod_im)) / length
    corr_im = (product_three(cosine_t, prod_im) + product_three(sine_t, prod_re)) / length
    factor = jnp.float32(energies) ** (-0.5)
    shaped = (energies, tail_shape[0], tail_shape[2], tail_shape[3])
    real_part = (corr_im * factor).reshape(shaped)
    imag_part = (-corr_re * factor).reshape(shaped)
    return jnp.stack([real_part, imag_part], axis=2).astype(jnp.bfloat16)


def left_plain(coupler, blocks):
    return jnp.einsum("ab,ecbd->ecad", coupler, blocks, preferred_element_type=jnp.float32).astype(
        jnp.bfloat16
    )


def left_transposed(coupler, blocks):
    return jnp.einsum("ba,ecbd->ecad", coupler, blocks, preferred_element_type=jnp.float32).astype(
        jnp.bfloat16
    )


def right_transposed(left, coupler):
    return jnp.einsum("ecad,fd->ecaf", left, coupler, preferred_element_type=jnp.float32)


def right_plain(left, coupler):
    return jnp.einsum("ecad,df->ecaf", left, coupler, preferred_element_type=jnp.float32)


def per_device(lesser, greater, coulomb_diag, coulomb_upper):
    greater_t = jnp.swapaxes(greater, 3, 4)
    lesser_x, greater_x = (
        lax.all_to_all(lesser, "energy", split_axis=3, concat_axis=0, tiled=True),
        lax.all_to_all(greater_t, "energy", split_axis=3, concat_axis=0, tiled=True),
    )
    polar_x = correlate(lesser_x, greater_x)
    polar = lax.all_to_all(polar_x, "energy", split_axis=0, concat_axis=3, tiled=True)
    own = polar[:, 0]
    diag_block = coulomb_diag[0]
    upper_block = coulomb_upper[0]
    total = right_transposed(left_plain(diag_block, own), diag_block)
    polar_next = from_behind(polar, "space", -1)
    outgoing = right_plain(left_transposed(upper_block, own), upper_block)
    total = total + right_transposed(left_plain(upper_block, polar_next[:, 0]), upper_block)
    incoming = from_behind(outgoing.astype(jnp.bfloat16), "space", 1).astype(outgoing.dtype)
    total = total + incoming
    return total.astype(jnp.bfloat16)[:, None]


GROUPS = 4
LAGS = 8
STEPS = 8
TILE = 16
LANES = 128
FILLER = 0
AHEAD = 2
BEHIND = 2
MESH = pl.DeviceIdType.MESH


def to_energy(dest):
    return {"energy": dest}


def to_space(dest):
    return {"space": dest}


def widen_into(held, block, values):
    count = values.shape[0]
    at = pl.ds(block * count, count)
    re, im = values[:, 0].astype(jnp.float32), values[:, 1].astype(jnp.float32)
    held[0, at] = re
    held[1, at] = im
    held[2, at] = re + im


def correlate_into(target, lf, hf, lag_block, size, begin, end):
    energies, rows = hf.shape[1], hf.shape[2]
    factor = float(energies) ** -0.5

    def one_slab(slab, carry):
        at = pl.ds(pl.multiple_of(slab * 8, 8), 8)
        for first in range(lag_block * size, (lag_block + 1) * size, LAGS):
            def step(turn, sums):
                start = turn * STEPS
                sums = list(sums)
                for q in range(3):
                    window = [lf[q, start + (first + t), at, :] for t in range(LAGS + STEPS - 1)]
                    taps = [hf[q, start + u, at, :] for u in range(STEPS)]
                    for u in range(STEPS):
                        for j in range(LAGS):
                            sums[q * LAGS + j] = sums[q * LAGS + j] + window[j + u] * taps[u]
                return tuple(sums)

            zero = jnp.zeros((8, LANES), jnp.float32)
            low = max(0, begin * size - first - (LAGS - 1)) // STEPS
            high = max(0, end * size - first) // STEPS
            sums = lax.fori_loop(low, high, step, (zero,) * (3 * LAGS))
            for j in range(LAGS):
                rr, ii, mixed = sums[j], sums[LAGS + j], sums[2 * LAGS + j]
                lag = first - lag_block * size + j
                target[lag, 0, at, :] = (mixed - rr - ii) * factor
                target[lag, 1, at, :] = (ii - rr) * factor
        return carry

    lax.fori_loop(0, rows // 8, one_slab, 0)


def kernel(
    n, ns, lesser, greater, diag_hbm, upper_hbm, out,
    diag, upper, lv, gv, ht, held, lf, hf, lff, cf, own_sum, cs, cin, polar, side, uprev, wside, total,
    local_sem, deal_send, deal_recv, z_send, z_recv, c_send, c_recv, back_send, back_recv,
    side_send, side_recv, u_send, u_recv, far,
):
    me = lax.axis_index("energy")
    row = lax.axis_index("space")
    pieces, _, groups, block, _, _, _ = held.shape
    chunks, k, _, size, _ = polar.shape
    members = n // groups
    share = size // members
    stacks = share // TILE
    plane, member = me // members, lax.rem(me, members)
    has_next = row < ns - 1
    has_prev = row > 0
    rest = [p for p in range(pieces) if p != FILLER]

    def column(level):
        return to_energy(level * members + member)

    barrier = pltpu.get_barrier_semaphore()

    def greet(step, carry):
        peer = plane * members + lax.rem(member + step, members)
        pl.semaphore_signal(barrier, inc=1, device_id=to_energy(peer), device_id_type=MESH)
        return carry

    lax.fori_loop(1, members, greet, 0)

    greeted = {0: (1,), 1: (0, 2, 3), 2: (1, 3), 3: ()}
    for level, others in greeted.items():
        if others:
            @pl.when(plane == level)
            def _():
                for other in others:
                    pl.semaphore_signal(barrier, inc=1, device_id=column(other), device_id_type=MESH)

    @pl.when(has_next)
    def _():
        pl.semaphore_signal(barrier, inc=1, device_id=to_space(row + 1), device_id_type=MESH)

    @pl.when(has_prev)
    def _():
        pl.semaphore_signal(barrier, inc=1, device_id=to_space(row - 1), device_id_type=MESH)

    load_g = pltpu.make_async_copy(greater.at[:, 0], gv, local_sem.at[0])
    load_g.start()
    load_l = pltpu.make_async_copy(lesser.at[:, 0], lv, local_sem.at[1])
    load_l.start()
    load_upper = pltpu.make_async_copy(upper_hbm, upper, local_sem.at[2])
    load_upper.start()
    load_diag = pltpu.make_async_copy(diag_hbm, diag, local_sem.at[3])
    load_diag.start()
    load_g.wait()
    for e in range(k):
        for part_at in range(2):
            ht[e, part_at] = gv[e, part_at].T
    lf[...] = jnp.zeros(lf.shape, jnp.float32)
    lff[...] = jnp.zeros(lff.shape, jnp.float32)
    load_l.wait()
    load_upper.wait()
    load_diag.wait()

    two = jnp.logical_or(plane == 1, plane == 3).astype(jnp.int32)
    pl.semaphore_wait(
        barrier, members + two + has_next.astype(jnp.int32) + has_prev.astype(jnp.int32)
    )

    @pl.when(plane == 1)
    def _():
        pl.semaphore_signal(far, inc=1, device_id=column(0), device_id_type=MESH)

    u_copy = pltpu.make_async_remote_copy(
        src_ref=upper_hbm.at[0], dst_ref=uprev, send_sem=u_send, recv_sem=u_recv,
        device_id=to_space(lax.rem(row + 1, ns)), device_id_type=MESH,
    )

    def share_rows(who, p):
        return pl.ds(pl.multiple_of(who * share + (p % stacks) * TILE, TILE), TILE)

    def energies_of(who):
        return pl.ds(pl.multiple_of(who * k, k), k)

    def deal(p, kind):
        source = (lv, ht)[kind]
        cols = pl.ds((p // stacks) * LANES, LANES)
        landing = held.at[p, kind, plane, energies_of(member)]

        def push(step, carry):
            peer = lax.rem(member + step, members)
            pltpu.make_async_remote_copy(
                src_ref=source.at[:, :, share_rows(peer, p), cols], dst_ref=landing,
                send_sem=deal_send.at[kind], recv_sem=deal_recv.at[kind, p],
                device_id=to_energy(plane * members + peer), device_id_type=MESH,
            ).start()
            return carry

        lax.fori_loop(1, members, push, 0)
        pltpu.make_async_copy(
            source.at[:, :, share_rows(member, p), cols], landing, deal_recv.at[kind, p]
        ).start()

    first = rest[0]

    @pl.when(plane < 2)
    def _():
        deal(first, 1)
        deal(FILLER, 1)
        deal(FILLER, 0)
        deal(first, 0)

    @pl.when(plane >= 2)
    def _():
        deal(FILLER, 0)
        deal(FILLER, 1)
        deal(first, 0)
        deal(first, 1)

    for p in rest[1:]:
        deal(p, 1)
        deal(p, 0)

    @pl.when(has_next)
    def _():
        u_copy.start()

    def settle(ref, sem):
        pltpu.make_async_copy(ref, ref, sem).wait()

    def dealt(p, kind, level):
        settle(held.at[p, kind, level], deal_recv.at[kind, p])

    def lift(p, kind, level, to):
        pltpu.make_async_remote_copy(
            src_ref=held.at[p, kind, level], dst_ref=held.at[p, kind, level], send_sem=z_send,
            recv_sem=z_recv.at[p], device_id=column(to), device_id_type=MESH,
        ).start()

    def give(p, lag_block, slot, to):
        pltpu.make_async_remote_copy(
            src_ref=cs.at[p, lag_block], dst_ref=cin.at[p, slot], send_sem=c_send.at[int(p == FILLER)],
            recv_sem=c_recv.at[p], device_id=column(to), device_id_type=MESH,
        ).start()

    def back(source, p):
        c = p // stacks
        landing = polar.at[c, :, :, share_rows(member, p), :]

        def push(step, carry):
            peer = lax.rem(member + step, members)
            pltpu.make_async_remote_copy(
                src_ref=source.at[energies_of(peer)], dst_ref=landing,
                send_sem=back_send, recv_sem=back_recv.at[c],
                device_id=to_energy(plane * members + peer), device_id_type=MESH,
            ).start()
            return carry

        lax.fori_loop(1, members, push, 0)
        pltpu.make_async_copy(source.at[energies_of(member)], landing, back_recv.at[c]).start()

    def screen(source, coupler, c, begin):
        right = coupler[:, c * LANES:(c + 1) * LANES]
        for e in range(k):
            pair = jnp.concatenate([source[e, 0], source[e, 1]], axis=1)
            left = jnp.dot(coupler, pair, preferred_element_type=jnp.float32).astype(jnp.bfloat16)
            for part_at in range(2):
                term = lax.dot_general(
                    left[:, part_at * LANES:(part_at + 1) * LANES], right,
                    (((1,), (1,)), ((), ())), preferred_element_type=jnp.float32,
                )
                if begin:
                    total[e, part_at] = term
                else:
                    total[e, part_at] += term

    up, down = lax.rem(row + 1, ns), lax.rem(row + ns - 1, ns)

    def forward(c, slot, to):
        return pltpu.make_async_remote_copy(
            src_ref=polar.at[c], dst_ref=side.at[slot, c], send_sem=side_send.at[slot, c],
            recv_sem=side_recv.at[slot, c], device_id=to_space(to), device_id_type=MESH,
        )

    def screen_own(c):
        settle(polar.at[c], back_recv.at[c])

        @pl.when(has_prev)
        def _():
            forward(c, 0, down).start()

        @pl.when(has_next)
        def _():
            forward(c, 1, up).start()

        screen(polar.at[c], diag[0], c, c == 0)

    def screen_sides(c):
        @pl.when(has_next)
        def _():
            forward(c, 0, down).wait_recv()
            screen(side.at[0, c], wside[0], c, False)

        @pl.when(has_prev)
        def _():
            forward(c, 1, up).wait_recv()
            screen(side.at[1, c], wside[1], c, False)

    def ready_couplers():
        wside[0] = upper[0]

        @pl.when(has_prev)
        def _():
            u_copy.wait_recv()
            wside[1] = uprev[...].T

    def middle(turn):
        c = (turn - BEHIND) // stacks - 1
        when = (turn - BEHIND) % stacks
        if 0 <= c < chunks - 1 and when == 1:
            if c == 0:
                ready_couplers()
            screen_own(c)
            screen_sides(c)

    def add(p, lag_block, slots):
        settle(cin.at[p, pl.ds(0, slots)], c_recv.at[p])
        value = own_sum[p]
        for slot in range(slots):
            value = value + cin[p, slot].astype(jnp.float32)
        cs[p, lag_block] = value.astype(jnp.bfloat16)
        back(cs.at[p, lag_block], p)

    def relay(p):
        settle(cin.at[p, 0], c_recv.at[p])
        back(cin.at[p, 0], p)

    turns = range(1, len(rest) + BEHIND + 1)
    meet = BEHIND + 2

    def at_turn(turn):
        return rest[turn - 1] if 1 <= turn <= len(rest) else None

    def rounded(p, lag_block):
        cs[p, lag_block] = cf[...].astype(jnp.bfloat16)

    @pl.when(plane == 0)
    def _():
        def send(p):
            dealt(p, 1, 0)
            if p != FILLER:
                lift(p, 1, 0, 2)
            lift(p, 1, 0, 1)

        pl.semaphore_wait(far, 1)
        send(first)
        send(FILLER)
        dealt(FILLER, 0, 0)
        lift(FILLER, 0, 0, 1)
        for turn in range(2, AHEAD + 1):
            send(at_turn(turn))
        for turn in turns:
            ahead, p, done = at_turn(turn + AHEAD), at_turn(turn), at_turn(turn - BEHIND)
            if ahead is not None:
                send(ahead)
            if p is not None:
                dealt(p, 0, 0)
                widen_into(lf, 0, held[p, 0, 0])
                widen_into(hf, 0, held[p, 1, 0])
                correlate_into(own_sum.at[p], lf, hf, 0, block, 0, 1)
            if turn == meet:
                relay(FILLER)
            if done is not None:
                add(done, 0, 2)
            middle(turn)

    @pl.when(plane == 1)
    def _():
        def send(p):
            dealt(p, 1, 1)
            lift(p, 1, 1, 2)

        for turn in range(1, AHEAD + 1):
            send(at_turn(turn))
        for turn in turns:
            ahead, p, done = at_turn(turn + AHEAD), at_turn(turn), at_turn(turn - BEHIND)
            if ahead is not None:
                send(ahead)
            if p is not None:
                dealt(p, 0, 1)
                widen_into(lf, 1, held[p, 0, 1])
                widen_into(hf, 1, held[p, 1, 1])
                settle(held.at[p, 1, 0], z_recv.at[p])
                widen_into(hf, 0, held[p, 1, 0])
                correlate_into(cf, lf, hf, 0, block, 1, 2)
                rounded(p, 0)
                give(p, 0, 0, 0)
                correlate_into(own_sum.at[p], lf, hf, 1, block, 1, 2)
            if turn == BEHIND:
                dealt(FILLER, 0, 1)
                dealt(FILLER, 1, 1)
                settle(held.at[FILLER, :, pl.ds(0, groups - 1)], z_recv.at[FILLER])
                for level in range(groups):
                    widen_into(lff, level, held[FILLER, 0, level])
                    widen_into(hf, level, held[FILLER, 1, level])
                for lag_block in (0, 2, 3, 1):
                    correlate_into(cf, lff, hf, lag_block, block, 0, groups)
                    rounded(FILLER, lag_block)
                    if lag_block == 1:
                        back(cs.at[FILLER, 1], FILLER)
                    else:
                        give(FILLER, lag_block, 0, lag_block)
            if done is not None:
                add(done, 1, 1)
            middle(turn)

    @pl.when(plane == 2)
    def _():
        dealt(FILLER, 0, 2)
        lift(FILLER, 0, 2, 1)
        dealt(FILLER, 1, 2)
        lift(FILLER, 1, 2, 1)
        for turn in turns:
            p = at_turn(turn)
            if p is not None:
                dealt(p, 0, 2)
                dealt(p, 1, 2)
                widen_into(lf, 2, held[p, 0, 2])
                widen_into(hf, 2, held[p, 1, 2])
                settle(held.at[p, 0, pl.ds(0, groups)], z_recv.at[p])
                widen_into(lf, 3, held[p, 0, 3])
                for level in (0, 1, 3):
                    widen_into(hf, level, held[p, 1, level])
                for lag_block in (0, 1, 3, 2):
                    correlate_into(cf, lf, hf, lag_block, block, 2, groups)
                    rounded(p, lag_block)
                    if lag_block == 2:
                        back(cs.at[p, 2], p)
                    else:
                        give(p, lag_block, 0 if lag_block == 1 or lag_block == 3 else 1, lag_block)
            if turn == meet:
                relay(FILLER)
            middle(turn)

    @pl.when(plane == 3)
    def _():
        def send(p, to):
            for kind in range(2):
                dealt(p, kind, 3)
                lift(p, kind, 3, to)

        send(first, 2)
        send(FILLER, 1)
        for p in rest[1:]:
            send(p, 2)
        for turn in turns:
            p = at_turn(turn)
            if p is not None:
                relay(p)
            if turn == meet:
                relay(FILLER)
            middle(turn)

    last = chunks - 1
    screen_own(last)
    screen_sides(last)
    out[:, 0] = total[...].astype(jnp.bfloat16)

    for c in range(chunks):
        @pl.when(has_prev)
        def _():
            forward(c, 0, down).wait_send()

        @pl.when(has_next)
        def _():
            forward(c, 1, up).wait_send()

    @pl.when(has_next)
    def _():
        u_copy.wait_send()

    for sem in (deal_send.at[0], deal_send.at[1], back_send):
        settle(held.at[:, 0, 0, pl.ds(0, k * (members - 1))], sem)

    others = pl.ds(0, len(rest))

    @pl.when(jnp.logical_or(plane == 0, plane == 3))
    def _():
        settle(held.at[:, 0, pl.ds(0, 2)], z_send)

    @pl.when(plane == 1)
    def _():
        settle(held.at[others, 0, 0], z_send)
        settle(cs.at[others, 0], c_send.at[0])
        settle(cs.at[0, pl.ds(0, 3)], c_send.at[1])

    @pl.when(plane == 2)
    def _():
        settle(held.at[0, 0, pl.ds(0, 2)], z_send)
        settle(cs.at[others, pl.ds(0, 3)], c_send.at[0])


def fused(n, ns, lesser, greater, diag, upper):
    k, _, _, size, _ = lesser.shape
    members, energies, chunks = n // GROUPS, n * k, size // LANES
    block = members * k
    pieces = chunks * (size // members // TILE)
    bf, f32 = jnp.bfloat16, jnp.float32
    whole = (k, 2, size, size)
    piece = (block, 2, TILE, LANES)
    padded = energies + LAGS + STEPS
    dma = pltpu.SemaphoreType.DMA
    vmem = pl.BlockSpec(memory_space=pltpu.VMEM)
    hbm = pl.BlockSpec(memory_space=pltpu.HBM)
    return pl.pallas_call(
        functools.partial(kernel, n, ns),
        out_shape=jax.ShapeDtypeStruct(lesser.shape, bf),
        in_specs=[hbm] * 4,
        out_specs=vmem,
        scratch_shapes=[
            pltpu.VMEM(diag.shape, bf),
            pltpu.VMEM(upper.shape, bf),
            pltpu.VMEM(whole, bf),
            pltpu.VMEM(whole, bf),
            pltpu.VMEM(whole, bf),
            pltpu.VMEM((pieces, 2, GROUPS) + piece, bf),
            pltpu.VMEM((3, padded, TILE, LANES), f32),
            pltpu.VMEM((3, energies, TILE, LANES), f32),
            pltpu.VMEM((3, padded, TILE, LANES), f32),
            pltpu.VMEM(piece, f32),
            pltpu.VMEM((pieces,) + piece, f32),
            pltpu.VMEM((pieces, GROUPS) + piece, bf),
            pltpu.VMEM((pieces, 2) + piece, bf),
            pltpu.VMEM((chunks, k, 2, size, LANES), bf),
            pltpu.VMEM((2, chunks, k, 2, size, LANES), bf),
            pltpu.VMEM((size, size), bf),
            pltpu.VMEM((2, size, size), bf),
            pltpu.VMEM(whole, f32),
            dma((4,)), dma((2,)), dma((2, pieces)), dma, dma((pieces,)), dma((2,)), dma((pieces,)),
            dma, dma((chunks,)), dma((2, chunks)), dma((2, chunks)), dma, dma,
            pltpu.SemaphoreType.REGULAR,
        ],
        compiler_params=pltpu.CompilerParams(
            collective_id=0, has_side_effects=True, vmem_limit_bytes=40 << 20
        ),
    )(*(pltpu.with_memory_space_constraint(x, pltpu.HBM) for x in (lesser, greater, diag, upper)))


def fits(n, ns, size, k):
    if n % GROUPS or size % LANES or size <= LANES or ns < 2:
        return False
    members = n // GROUPS
    if members < 2 or size % (members * TILE) or (members * k) % STEPS:
        return False
    stacks = size // members // TILE
    return 2 <= stacks and size // LANES * stacks <= 16


def either(n, ns, lesser, greater, diag, upper):
    if fits(n, ns, lesser.shape[3], lesser.shape[0]):
        return fused(n, ns, lesser, greater, diag, upper)
    return per_device(lesser, greater, diag, upper)


def solution(mesh):
    placed = (
        P("energy", "space", None, None, None),
        P("energy", "space", None, None, None),
        P("space", None, None),
        P("space", None, None),
    )
    return jax.shard_map(
        functools.partial(either, mesh.shape["energy"], mesh.shape["space"]),
        mesh=mesh,
        in_specs=placed,
        out_specs=P("energy", "space", None, None, None),
        check_vma=False,
    )
```

```python
import functools
import math

import jax
import jax.numpy as jnp
from jax import lax
from jax.experimental import pallas as pl
from jax.experimental.pallas import tpu as pltpu
from jax.sharding import PartitionSpec as P


def from_behind(value, axis, steps):
    count = lax.axis_size(axis)
    leading, last = (max(0, -steps), min(count, count - steps))
    return lax.ppermute(value, axis, [(source, source + steps) for source in range(leading, last)])


def split_parts(values):
    high = values.astype(jnp.bfloat16)
    low = (values - high.astype(jnp.float32)).astype(jnp.bfloat16)
    return (high, low)


def product_two(table, data_bf):
    return jnp.dot(table[0], data_bf, preferred_element_type=jnp.float32) + jnp.dot(
        table[1], data_bf, preferred_element_type=jnp.float32
    )


def product_three(table, data_f32):
    data_high, data_low = split_parts(data_f32)
    total = jnp.dot(table[0], data_high, preferred_element_type=jnp.float32)
    total = total + jnp.dot(table[1], data_high, preferred_element_type=jnp.float32)
    return total + jnp.dot(table[0], data_low, preferred_element_type=jnp.float32)


def correlate(lesser_x, greater_x):
    energies = lesser_x.shape[0]
    length = 2 * energies
    tail_shape = lesser_x.shape[1:]

    def flatten(values, part):
        return values[:, :, part].reshape(energies, -1)

    lesser_re = flatten(lesser_x, 0)
    lesser_im = flatten(lesser_x, 1)
    greater_re = flatten(greater_x, 0)
    greater_im = flatten(greater_x, 1)
    freqs = lax.broadcasted_iota(jnp.int32, (length, energies), 0)
    places = lax.broadcasted_iota(jnp.int32, (length, energies), 1)
    angles = 2.0 * math.pi / length * jnp.mod(freqs * places, length).astype(jnp.float32)
    cosine = split_parts(jnp.cos(angles))
    sine = split_parts(jnp.sin(angles))
    cosine_t = split_parts(jnp.cos(angles).T)
    sine_t = split_parts(jnp.sin(angles).T)
    hat_lre = product_two(cosine, lesser_re) + product_two(sine, lesser_im)
    hat_lim = product_two(cosine, lesser_im) - product_two(sine, lesser_re)
    hat_gre = product_two(cosine, greater_re) - product_two(sine, greater_im)
    hat_gim = product_two(cosine, greater_im) + product_two(sine, greater_re)
    prod_re = hat_lre * hat_gre - hat_lim * hat_gim
    prod_im = hat_lre * hat_gim + hat_lim * hat_gre
    corr_re = (product_three(cosine_t, prod_re) - product_three(sine_t, prod_im)) / length
    corr_im = (product_three(cosine_t, prod_im) + product_three(sine_t, prod_re)) / length
    factor = jnp.float32(energies) ** (-0.5)
    shaped = (energies, tail_shape[0], tail_shape[2], tail_shape[3])
    real_part = (corr_im * factor).reshape(shaped)
    imag_part = (-corr_re * factor).reshape(shaped)
    return jnp.stack([real_part, imag_part], axis=2).astype(jnp.bfloat16)


def left_plain(coupler, blocks):
    return jnp.einsum("ab,ecbd->ecad", coupler, blocks, preferred_element_type=jnp.float32).astype(
        jnp.bfloat16
    )


def left_transposed(coupler, blocks):
    return jnp.einsum("ba,ecbd->ecad", coupler, blocks, preferred_element_type=jnp.float32).astype(
        jnp.bfloat16
    )


def right_transposed(left, coupler):
    return jnp.einsum("ecad,fd->ecaf", left, coupler, preferred_element_type=jnp.float32)


def right_plain(left, coupler):
    return jnp.einsum("ecad,df->ecaf", left, coupler, preferred_element_type=jnp.float32)


def per_device(lesser, greater, coulomb_diag, coulomb_upper):
    greater_t = jnp.swapaxes(greater, 3, 4)
    lesser_x, greater_x = (
        lax.all_to_all(lesser, "energy", split_axis=3, concat_axis=0, tiled=True),
        lax.all_to_all(greater_t, "energy", split_axis=3, concat_axis=0, tiled=True),
    )
    polar_x = correlate(lesser_x, greater_x)
    polar = lax.all_to_all(polar_x, "energy", split_axis=0, concat_axis=3, tiled=True)
    own = polar[:, 0]
    diag_block = coulomb_diag[0]
    upper_block = coulomb_upper[0]
    total = right_transposed(left_plain(diag_block, own), diag_block)
    polar_next = from_behind(polar, "space", -1)
    outgoing = right_plain(left_transposed(upper_block, own), upper_block)
    total = total + right_transposed(left_plain(upper_block, polar_next[:, 0]), upper_block)
    incoming = from_behind(outgoing.astype(jnp.bfloat16), "space", 1).astype(outgoing.dtype)
    total = total + incoming
    return total.astype(jnp.bfloat16)[:, None]


GROUPS = 4
LAGS = 8
STEPS = 8
TILE = 16
LANES = 128
AHEAD = 4
STRAIGHT = 2
LATE = 1
FIRST = 3
MESH = pl.DeviceIdType.MESH


def to_energy(dest):
    return {"energy": dest}


def to_space(dest):
    return {"space": dest}


def widen_into(held, block, values):
    count = values.shape[0]
    at = pl.ds(block * count, count)
    re, im = values[:, 0].astype(jnp.float32), values[:, 1].astype(jnp.float32)
    held[0, at] = re
    held[1, at] = im
    held[2, at] = re + im


def correlate_into(target, lf, hf, lag_block, size, begin, end):
    energies, rows = hf.shape[1], hf.shape[2]
    factor = float(energies) ** -0.5

    def one_slab(slab, carry):
        at = pl.ds(pl.multiple_of(slab * 8, 8), 8)
        for first in range(lag_block * size, (lag_block + 1) * size, LAGS):
            def step(turn, sums):
                start = turn * STEPS
                sums = list(sums)
                for q in range(3):
                    window = [lf[q, start + (first + t), at, :] for t in range(LAGS + STEPS - 1)]
                    taps = [hf[q, start + u, at, :] for u in range(STEPS)]
                    for u in range(STEPS):
                        for j in range(LAGS):
                            sums[q * LAGS + j] = sums[q * LAGS + j] + window[j + u] * taps[u]
                return tuple(sums)

            zero = jnp.zeros((8, LANES), jnp.float32)
            low = max(0, begin * size - first - (LAGS - 1)) // STEPS
            high = max(0, end * size - first) // STEPS
            sums = lax.fori_loop(low, high, step, (zero,) * (3 * LAGS))
            for j in range(LAGS):
                rr, ii, mixed = sums[j], sums[LAGS + j], sums[2 * LAGS + j]
                lag = first - lag_block * size + j
                target[lag, 0, at, :] = (mixed - rr - ii) * factor
                target[lag, 1, at, :] = (ii - rr) * factor
        return carry

    lax.fori_loop(0, rows // 8, one_slab, 0)


def kernel(
    n, ns, lesser, greater, diag_hbm, upper_hbm, out,
    diag, upper, gv, ht, held, lf, hf, cf, own_sum, cs, cin, late, polar, side, uprev, wside, total,
    local_sem, deal_send, deal_recv, z_send, z_recv, h_recv, c_send, c_recv, late_recv, back_send, back_recv,
    side_send, side_recv, u_send, u_recv,
):
    me = lax.axis_index("energy")
    row = lax.axis_index("space")
    pieces, _, groups, block, _, _, _ = held.shape
    chunks, k, _, size, _ = polar.shape
    members = n // groups
    stack = members * TILE
    stacks = size // stack
    plane, member = me // members, lax.rem(me, members)
    has_next = row < ns - 1
    has_prev = row > 0
    straight_in = range(STRAIGHT)
    straight_out = range(pieces - STRAIGHT, pieces)

    def column(level):
        return to_energy(level * members + member)

    barrier = pltpu.get_barrier_semaphore()

    def greet(step, carry):
        peer = plane * members + lax.rem(member + step, members)
        pl.semaphore_signal(barrier, inc=1, device_id=to_energy(peer), device_id_type=MESH)
        return carry

    lax.fori_loop(1, members, greet, 0)

    @pl.when(plane == 0)
    def _():
        pl.semaphore_signal(barrier, inc=1, device_id=column(2), device_id_type=MESH)

    @pl.when(plane == 1)
    def _():
        pl.semaphore_signal(barrier, inc=1, device_id=column(0), device_id_type=MESH)

    @pl.when(plane == 2)
    def _():
        pl.semaphore_signal(barrier, inc=1, device_id=column(1), device_id_type=MESH)
        for peer in range(members):
            pl.semaphore_signal(barrier, inc=1, device_id=to_energy(3 * members + peer), device_id_type=MESH)

    @pl.when(has_next)
    def _():
        pl.semaphore_signal(barrier, inc=1, device_id=to_space(row + 1), device_id_type=MESH)

    @pl.when(has_prev)
    def _():
        pl.semaphore_signal(barrier, inc=1, device_id=to_space(row - 1), device_id_type=MESH)

    def load(c):
        rows = pl.ds(c * LANES, LANES)
        return pltpu.make_async_copy(greater.at[:, 0, :, rows, :], gv.at[:, :, rows, :], local_sem.at[c])

    for c in range(chunks):
        load(c).start()

    def turn_over(c):
        load(c).wait()
        cols = slice(c * LANES, (c + 1) * LANES)
        for e in range(k):
            for part_at in range(2):
                ht[e, part_at, :, cols] = gv[e, part_at, cols, :].T

    @pl.when(plane < 2)
    def _():
        turn_over(0)

    more_greet = (members - 1) * (plane == 3).astype(jnp.int32)
    pl.semaphore_wait(
        barrier, members + more_greet + has_next.astype(jnp.int32) + has_prev.astype(jnp.int32)
    )

    u_copy = pltpu.make_async_remote_copy(
        src_ref=upper_hbm.at[0], dst_ref=uprev, send_sem=u_send, recv_sem=u_recv,
        device_id=to_space(lax.rem(row + 1, ns)), device_id_type=MESH,
    )

    def tile_of(who):
        return pl.ds(pl.multiple_of(who * TILE, TILE), TILE)

    def share_rows(who, p):
        return pl.ds(pl.multiple_of((p % stacks) * stack + who * TILE, TILE), TILE)

    def piece_rows(p):
        return pl.ds((p % stacks) * stack, stack)

    def energies_of(who):
        return pl.ds(pl.multiple_of(who * k, k), k)

    def part(p, kind, who):
        source = (lesser.at[:, 0], ht)[kind]
        return source.at[:, :, share_rows(who, p), pl.ds((p // stacks) * LANES, LANES)]

    def deal(p, kind):
        landing = held.at[p, kind, plane, energies_of(member)]

        def push(step, carry):
            peer = lax.rem(member + step, members)
            pltpu.make_async_remote_copy(
                src_ref=part(p, kind, peer), dst_ref=landing,
                send_sem=deal_send.at[kind], recv_sem=deal_recv.at[kind, p],
                device_id=to_energy(plane * members + peer), device_id_type=MESH,
            ).start()
            return carry

        lax.fori_loop(1, members, push, 0)
        pltpu.make_async_copy(part(p, kind, member), landing, deal_recv.at[kind, p]).start()

    def drop(p, kind):
        def push(step, carry):
            peer = lax.rem(member + step, members)
            pltpu.make_async_remote_copy(
                src_ref=part(p, kind, peer), dst_ref=held.at[p, kind, 3, energies_of(member)],
                send_sem=z_send, recv_sem=z_recv.at[p],
                device_id=to_energy(2 * members + peer), device_id_type=MESH,
            ).start()
            return carry

        lax.fori_loop(0, members, push, 0)

    lead = min(AHEAD, pieces)

    @pl.when(plane < 2)
    def _():
        for p in range(lead):
            deal(p, 1)

    @pl.when(plane == 2)
    def _():
        deal(0, 0)
        turn_over(0)
        deal(0, 1)

    @pl.when(plane == 3)
    def _():
        drop(0, 0)
        turn_over(0)
        drop(0, 1)

    for c in range(1, chunks):
        turn_over(c)

    @pl.when(plane < 2)
    def _():
        for p in range(pieces):
            deal(p, 0)
            if p + lead < pieces:
                deal(p + lead, 1)

    @pl.when(plane == 2)
    def _():
        for p in range(1, pieces):
            deal(p, 0)
            deal(p, 1)

    @pl.when(plane == 3)
    def _():
        for p in range(1, pieces):
            for kind in range(2):
                if p in straight_in:
                    drop(p, kind)
                else:
                    deal(p, kind)

    load_upper = pltpu.make_async_copy(upper_hbm, upper, local_sem.at[chunks])
    load_upper.start()
    load_diag = pltpu.make_async_copy(diag_hbm, diag, local_sem.at[chunks + 1])
    load_diag.start()
    lf[...] = jnp.zeros(lf.shape, jnp.float32)

    @pl.when(has_next)
    def _():
        u_copy.start()

    def settle(ref, sem):
        pltpu.make_async_copy(ref, ref, sem).wait()

    def dealt(p, kind, level):
        settle(held.at[p, kind, level], deal_recv.at[kind, p])

    def lift(p, kind, level, to, recv):
        pltpu.make_async_remote_copy(
            src_ref=held.at[p, kind, level], dst_ref=held.at[p, kind, level], send_sem=z_send,
            recv_sem=recv.at[p], device_id=column(to), device_id_type=MESH,
        ).start()

    def give(p, lag_block, slot):
        pltpu.make_async_remote_copy(
            src_ref=cs.at[p, lag_block], dst_ref=cin.at[p, slot], send_sem=c_send,
            recv_sem=c_recv.at[p], device_id=column(lag_block), device_id_type=MESH,
        ).start()

    def give_straight(p, lag_block):
        at = p - straight_out[0]

        def push(step, carry):
            peer = lax.rem(member + step, members)
            pltpu.make_async_remote_copy(
                src_ref=cs.at[p, lag_block, energies_of(peer)], dst_ref=late.at[at, :, :, tile_of(member), :],
                send_sem=c_send, recv_sem=late_recv.at[at],
                device_id=to_energy(lag_block * members + peer), device_id_type=MESH,
            ).start()
            return carry

        lax.fori_loop(0, members, push, 0)

    def back(source, p):
        landing = polar.at[p // stacks, :, :, share_rows(member, p), :]

        def push(step, carry):
            peer = lax.rem(member + step, members)
            pltpu.make_async_remote_copy(
                src_ref=source.at[energies_of(peer)], dst_ref=landing,
                send_sem=back_send, recv_sem=back_recv.at[p],
                device_id=to_energy(plane * members + peer), device_id_type=MESH,
            ).start()
            return carry

        lax.fori_loop(1, members, push, 0)
        pltpu.make_async_copy(source.at[energies_of(member)], landing, back_recv.at[p]).start()

    def terms(source, coupler, c):
        right = coupler[:, c * LANES:(c + 1) * LANES]
        for e in range(k):
            pair = jnp.concatenate([source[e, 0], source[e, 1]], axis=1)
            left = jnp.dot(coupler, pair, preferred_element_type=jnp.float32).astype(jnp.bfloat16)
            for part_at in range(2):
                yield e, part_at, lax.dot_general(
                    left[:, part_at * LANES:(part_at + 1) * LANES], right,
                    (((1,), (1,)), ((), ())), preferred_element_type=jnp.float32,
                )

    def screen(source, coupler, c, begin):
        for e, part_at, term in terms(source, coupler, c):
            if begin:
                total[e, part_at] = term
            else:
                total[e, part_at] += term

    def finish(source, coupler, c):
        for e, part_at, term in terms(source, coupler, c):
            out[e, 0, part_at] = (total[e, part_at] + term).astype(jnp.bfloat16)

    up, down = lax.rem(row + 1, ns), lax.rem(row + ns - 1, ns)

    def forward(p, slot, to):
        place = (p // stacks, slice(None), slice(None), piece_rows(p))
        return pltpu.make_async_remote_copy(
            src_ref=polar.at[place], dst_ref=side.at[(slot,) + place], send_sem=side_send.at[slot],
            recv_sem=side_recv.at[slot, p // stacks], device_id=to_space(to), device_id_type=MESH,
        )

    def hand_over(p):
        place = (p // stacks, slice(None), slice(None), piece_rows(p))
        settle(polar.at[place], back_recv.at[p])
        if p in straight_out:
            @pl.when(plane < 2)
            def _():
                at = p - straight_out[0]
                settle(late.at[at], late_recv.at[at])
                both = polar[place].astype(jnp.float32) + late[at].astype(jnp.float32)
                polar[place] = both.astype(jnp.bfloat16)

        @pl.when(has_prev)
        def _():
            forward(p, 0, down).start()

        @pl.when(has_next)
        def _():
            forward(p, 1, up).start()

    def screen_own(c):
        for p in range(c * stacks, (c + 1) * stacks):
            hand_over(p)
        screen(polar.at[c], diag[0], c, c == 0)

    def from_next(c, act):
        @pl.when(has_next)
        def _():
            settle(side.at[0, c], side_recv.at[0, c])
            act(side.at[0, c], wside[0], c)

    def from_prev(c, act):
        @pl.when(has_prev)
        def _():
            settle(side.at[1, c], side_recv.at[1, c])
            act(side.at[1, c], wside[1], c)

    def more(source, coupler, c):
        screen(source, coupler, c, False)

    def screen_sides(c):
        from_next(c, more)
        from_prev(c, more)

    def couplers():
        load_upper.wait()
        load_diag.wait()
        wside[0] = upper[0]

        @pl.when(has_prev)
        def _():
            u_copy.wait_recv()
            wside[1] = uprev[...].T

    def middle(p):
        c = (p - 1) // stacks - 1
        if 0 <= c < chunks - 1 and (p - 1) % stacks == 0:
            if c == 0:
                couplers()
            screen_own(c)

    def add(p, lag_block, slots):
        value = own_sum[p]
        if slots:
            settle(cin.at[p, pl.ds(0, slots)], c_recv.at[p])
        for slot in range(slots):
            value = value + cin[p, slot].astype(jnp.float32)
        cs[p, lag_block] = value.astype(jnp.bfloat16)
        back(cs.at[p, lag_block], p)

    def rounded(p, lag_block):
        cs[p, lag_block] = cf[...].astype(jnp.bfloat16)

    early = list(range(max(0, stacks - 1)))
    order = early + list(straight_out) + [p for p in range(pieces) if p not in early and p not in straight_out]

    @pl.when(plane == 0)
    def _():
        def send(p):
            dealt(p, 1, 0)
            lift(p, 1, 0, 1, h_recv)

        for p in range(pieces):
            send(p)
        for p in range(pieces):
            dealt(p, 0, 0)
            widen_into(lf, 0, held[p, 0, 0])
            widen_into(hf, 0, held[p, 1, 0])
            correlate_into(own_sum.at[p], lf, hf, 0, block, 0, 1)
        for p in order:
            add(p, 0, 1 if p in straight_out else 2)
            middle(p)

    @pl.when(plane == 1)
    def _():
        def send(p):
            dealt(p, 1, 1)
            lift(p, 1, 1, 2, z_recv)

        for p in range(FIRST):
            send(p)
        held_back = []
        for p in range(pieces):
            settle(held.at[p, 1, 0], h_recv.at[p])
            lift(p, 1, 0, 2, h_recv)
            if p + FIRST < pieces:
                send(p + FIRST)
            dealt(p, 0, 1)
            widen_into(lf, 1, held[p, 0, 1])
            widen_into(hf, 1, held[p, 1, 1])
            widen_into(hf, 0, held[p, 1, 0])
            correlate_into(cf, lf, hf, 0, block, 1, 2)
            rounded(p, 0)
            if p in early or p in straight_out:
                give(p, 0, 0)
            else:
                held_back.append(p)
            correlate_into(own_sum.at[p], lf, hf, 1, block, 1, 2)
        for p in held_back:
            give(p, 0, 0)
        for p in order:
            add(p, 1, 0 if p in straight_out else 1)
            middle(p)

    @pl.when(plane == 2)
    def _():
        def share(p, lag_block):
            if p in straight_out:
                give_straight(p, lag_block)
            else:
                give(p, lag_block, 1 - lag_block)

        waiting = []
        for p in range(pieces):
            dealt(p, 0, 2)
            dealt(p, 1, 2)
            widen_into(lf, 2, held[p, 0, 2])
            widen_into(hf, 2, held[p, 1, 2])
            settle(held.at[p, 0, pl.ds(0, 3)], z_recv.at[p])
            widen_into(lf, 3, held[p, 0, 3])
            widen_into(hf, 3, held[p, 1, 3])
            widen_into(hf, 1, held[p, 1, 1])
            correlate_into(cf, lf, hf, 0, block, 2, groups)
            rounded(p, 0)
            share(p, 0)
            for other in waiting:
                share(other, 1)
            waiting = []
            settle(held.at[p, 1, 0], h_recv.at[p])
            widen_into(hf, 0, held[p, 1, 0])
            correlate_into(cf, lf, hf, 1, block, 2, groups)
            rounded(p, 1)
            if pieces - 1 - LATE <= p < pieces - 1:
                waiting.append(p)
            else:
                share(p, 1)
            correlate_into(cf, lf, hf, 3, block, 2, groups)
            rounded(p, 3)
            give(p, 3, 0)
            correlate_into(cf, lf, hf, 2, block, 2, groups)
            rounded(p, 2)
            back(cs.at[p, 2], p)
            middle(p)

    @pl.when(plane == 3)
    def _():
        for p in range(pieces):
            if p not in straight_in:
                for kind in range(2):
                    dealt(p, kind, 3)
                    lift(p, kind, 3, 2, z_recv)
        for p in range(pieces):
            settle(cin.at[p, 0], c_recv.at[p])
            back(cin.at[p, 0], p)
            middle(p)

    for c in range(chunks - 1):
        screen_sides(c)
    last = chunks - 1
    screen_own(last)

    @pl.when(jnp.logical_and(has_prev, has_next))
    def _():
        from_next(last, more)

    @pl.when(has_prev)
    def _():
        settle(side.at[1, last], side_recv.at[1, last])
        finish(side.at[1, last], wside[1], last)

    @pl.when(row == 0)
    def _():
        settle(side.at[0, last], side_recv.at[0, last])
        finish(side.at[0, last], wside[0], last)

    @pl.when(has_prev)
    def _():
        settle(polar, side_send.at[0])

    @pl.when(has_next)
    def _():
        settle(polar, side_send.at[1])
        u_copy.wait_send()

    others = pl.ds(0, k * (members - 1))
    settle(held.at[:, 0, 0, others], back_send)

    @pl.when(plane < 3)
    def _():
        for kind in range(2):
            settle(held.at[:, kind, 0, others], deal_send.at[kind])

    @pl.when(plane == 0)
    def _():
        settle(held.at[:, 0, 0], z_send)

    @pl.when(plane == 1)
    def _():
        settle(held.at[:, 0, pl.ds(0, 2)], z_send)
        settle(cs.at[:, 0], c_send)

    @pl.when(plane == 2)
    def _():
        settle(cs.at[:, pl.ds(0, 3)], c_send)

    @pl.when(plane == 3)
    def _():
        settle(held.at[:, 0, pl.ds(0, 2)], z_send)
        for kind in range(2):
            settle(held.at[pl.ds(0, pieces - STRAIGHT), kind, 0, others], deal_send.at[kind])


def fused(n, ns, lesser, greater, diag, upper):
    k, _, _, size, _ = lesser.shape
    members, energies, chunks = n // GROUPS, n * k, size // LANES
    block = members * k
    pieces = chunks * (size // members // TILE)
    bf, f32 = jnp.bfloat16, jnp.float32
    whole = (k, 2, size, size)
    piece = (block, 2, TILE, LANES)
    padded = energies + LAGS + STEPS
    dma = pltpu.SemaphoreType.DMA
    vmem = pl.BlockSpec(memory_space=pltpu.VMEM)
    hbm = pl.BlockSpec(memory_space=pltpu.HBM)
    return pl.pallas_call(
        functools.partial(kernel, n, ns),
        out_shape=jax.ShapeDtypeStruct(lesser.shape, bf),
        in_specs=[hbm] * 4,
        out_specs=vmem,
        scratch_shapes=[
            pltpu.VMEM(diag.shape, bf),
            pltpu.VMEM(upper.shape, bf),
            pltpu.VMEM(whole, bf),
            pltpu.VMEM(whole, bf),
            pltpu.VMEM((pieces, 2, GROUPS) + piece, bf),
            pltpu.VMEM((3, padded, TILE, LANES), f32),
            pltpu.VMEM((3, energies, TILE, LANES), f32),
            pltpu.VMEM(piece, f32),
            pltpu.VMEM((pieces,) + piece, f32),
            pltpu.VMEM((pieces, GROUPS) + piece, bf),
            pltpu.VMEM((pieces, 2) + piece, bf),
            pltpu.VMEM((STRAIGHT, k, 2, members * TILE, LANES), bf),
            pltpu.VMEM((chunks, k, 2, size, LANES), bf),
            pltpu.VMEM((2, chunks, k, 2, size, LANES), bf),
            pltpu.VMEM((size, size), bf),
            pltpu.VMEM((2, size, size), bf),
            pltpu.VMEM(whole, f32),
            dma((chunks + 2,)), dma((2,)), dma((2, pieces)), dma, dma((pieces,)), dma((pieces,)), dma,
            dma((pieces,)), dma((STRAIGHT,)), dma, dma((pieces,)), dma((2,)), dma((2, chunks)), dma, dma,
        ],
        compiler_params=pltpu.CompilerParams(
            collective_id=0, has_side_effects=True, vmem_limit_bytes=40 << 20
        ),
    )(*(pltpu.with_memory_space_constraint(x, pltpu.HBM) for x in (lesser, greater, diag, upper)))


def fits(n, ns, size, k):
    if n % GROUPS or size % LANES or size <= LANES or ns < 2:
        return False
    members = n // GROUPS
    if members < 2 or size % (members * TILE) or (members * k) % STEPS:
        return False
    stacks = size // members // TILE
    return 2 <= stacks and 2 * STRAIGHT <= size // LANES * stacks <= 16


def either(n, ns, lesser, greater, diag, upper):
    if fits(n, ns, lesser.shape[3], lesser.shape[0]):
        return fused(n, ns, lesser, greater, diag, upper)
    return per_device(lesser, greater, diag, upper)


def solution(mesh):
    placed = (
        P("energy", "space", None, None, None),
        P("energy", "space", None, None, None),
        P("space", None, None),
        P("space", None, None),
    )
    return jax.shard_map(
        functools.partial(either, mesh.shape["energy"], mesh.shape["space"]),
        mesh=mesh,
        in_specs=placed,
        out_specs=P("energy", "space", None, None, None),
        check_vma=False,
    )
```

```python
import functools
import math

import jax
import jax.numpy as jnp
from jax import lax
from jax.experimental import pallas as pl
from jax.experimental.pallas import tpu as pltpu
from jax.sharding import PartitionSpec as P


def from_behind(value, axis, steps):
    count = lax.axis_size(axis)
    leading, last = (max(0, -steps), min(count, count - steps))
    return lax.ppermute(value, axis, [(source, source + steps) for source in range(leading, last)])


def split_parts(values):
    high = values.astype(jnp.bfloat16)
    low = (values - high.astype(jnp.float32)).astype(jnp.bfloat16)
    return (high, low)


def product_two(table, data_bf):
    return jnp.dot(table[0], data_bf, preferred_element_type=jnp.float32) + jnp.dot(
        table[1], data_bf, preferred_element_type=jnp.float32
    )


def product_three(table, data_f32):
    data_high, data_low = split_parts(data_f32)
    total = jnp.dot(table[0], data_high, preferred_element_type=jnp.float32)
    total = total + jnp.dot(table[1], data_high, preferred_element_type=jnp.float32)
    return total + jnp.dot(table[0], data_low, preferred_element_type=jnp.float32)


def correlate(lesser_x, greater_x):
    energies = lesser_x.shape[0]
    length = 2 * energies
    tail_shape = lesser_x.shape[1:]

    def flatten(values, part):
        return values[:, :, part].reshape(energies, -1)

    lesser_re = flatten(lesser_x, 0)
    lesser_im = flatten(lesser_x, 1)
    greater_re = flatten(greater_x, 0)
    greater_im = flatten(greater_x, 1)
    freqs = lax.broadcasted_iota(jnp.int32, (length, energies), 0)
    places = lax.broadcasted_iota(jnp.int32, (length, energies), 1)
    angles = 2.0 * math.pi / length * jnp.mod(freqs * places, length).astype(jnp.float32)
    cosine = split_parts(jnp.cos(angles))
    sine = split_parts(jnp.sin(angles))
    cosine_t = split_parts(jnp.cos(angles).T)
    sine_t = split_parts(jnp.sin(angles).T)
    hat_lre = product_two(cosine, lesser_re) + product_two(sine, lesser_im)
    hat_lim = product_two(cosine, lesser_im) - product_two(sine, lesser_re)
    hat_gre = product_two(cosine, greater_re) - product_two(sine, greater_im)
    hat_gim = product_two(cosine, greater_im) + product_two(sine, greater_re)
    prod_re = hat_lre * hat_gre - hat_lim * hat_gim
    prod_im = hat_lre * hat_gim + hat_lim * hat_gre
    corr_re = (product_three(cosine_t, prod_re) - product_three(sine_t, prod_im)) / length
    corr_im = (product_three(cosine_t, prod_im) + product_three(sine_t, prod_re)) / length
    factor = jnp.float32(energies) ** (-0.5)
    shaped = (energies, tail_shape[0], tail_shape[2], tail_shape[3])
    real_part = (corr_im * factor).reshape(shaped)
    imag_part = (-corr_re * factor).reshape(shaped)
    return jnp.stack([real_part, imag_part], axis=2).astype(jnp.bfloat16)


def left_plain(coupler, blocks):
    return jnp.einsum("ab,ecbd->ecad", coupler, blocks, preferred_element_type=jnp.float32).astype(
        jnp.bfloat16
    )


def left_transposed(coupler, blocks):
    return jnp.einsum("ba,ecbd->ecad", coupler, blocks, preferred_element_type=jnp.float32).astype(
        jnp.bfloat16
    )


def right_transposed(left, coupler):
    return jnp.einsum("ecad,fd->ecaf", left, coupler, preferred_element_type=jnp.float32)


def right_plain(left, coupler):
    return jnp.einsum("ecad,df->ecaf", left, coupler, preferred_element_type=jnp.float32)


def per_device(lesser, greater, coulomb_diag, coulomb_upper):
    greater_t = jnp.swapaxes(greater, 3, 4)
    lesser_x, greater_x = (
        lax.all_to_all(lesser, "energy", split_axis=3, concat_axis=0, tiled=True),
        lax.all_to_all(greater_t, "energy", split_axis=3, concat_axis=0, tiled=True),
    )
    polar_x = correlate(lesser_x, greater_x)
    polar = lax.all_to_all(polar_x, "energy", split_axis=0, concat_axis=3, tiled=True)
    own = polar[:, 0]
    diag_block = coulomb_diag[0]
    upper_block = coulomb_upper[0]
    total = right_transposed(left_plain(diag_block, own), diag_block)
    polar_next = from_behind(polar, "space", -1)
    outgoing = right_plain(left_transposed(upper_block, own), upper_block)
    total = total + right_transposed(left_plain(upper_block, polar_next[:, 0]), upper_block)
    incoming = from_behind(outgoing.astype(jnp.bfloat16), "space", 1).astype(outgoing.dtype)
    total = total + incoming
    return total.astype(jnp.bfloat16)[:, None]


GROUPS = 4
LAGS = 8
STEPS = 8
TILE = 16
LANES = 128
AHEAD = 4
STRAIGHT_IN = 2
STRAIGHT_OUT = 3
EARLY = 2
FIRST = 2
MESH = pl.DeviceIdType.MESH


def to_energy(dest):
    return {"energy": dest}


def to_space(dest):
    return {"space": dest}


def widen_into(held, block, values):
    count = values.shape[0]
    at = pl.ds(block * count, count)
    re, im = values[:, 0].astype(jnp.float32), values[:, 1].astype(jnp.float32)
    held[0, at] = re
    held[1, at] = im
    held[2, at] = re + im


def correlate_into(target, lf, hf, lag_block, size, begin, end):
    energies, rows = hf.shape[1], hf.shape[2]
    factor = float(energies) ** -0.5

    def one_slab(slab, carry):
        at = pl.ds(pl.multiple_of(slab * 8, 8), 8)
        for first in range(lag_block * size, (lag_block + 1) * size, LAGS):
            def step(turn, sums):
                start = turn * STEPS
                sums = list(sums)
                for q in range(3):
                    window = [lf[q, start + (first + t), at, :] for t in range(LAGS + STEPS - 1)]
                    taps = [hf[q, start + u, at, :] for u in range(STEPS)]
                    for u in range(STEPS):
                        for j in range(LAGS):
                            sums[q * LAGS + j] = sums[q * LAGS + j] + window[j + u] * taps[u]
                return tuple(sums)

            zero = jnp.zeros((8, LANES), jnp.float32)
            low = max(0, begin * size - first - (LAGS - 1)) // STEPS
            high = max(0, end * size - first) // STEPS
            sums = lax.fori_loop(low, high, step, (zero,) * (3 * LAGS))
            for j in range(LAGS):
                rr, ii, mixed = sums[j], sums[LAGS + j], sums[2 * LAGS + j]
                lag = first - lag_block * size + j
                target[lag, 0, at, :] = (mixed - rr - ii) * factor
                target[lag, 1, at, :] = (ii - rr) * factor
        return carry

    lax.fori_loop(0, rows // 8, one_slab, 0)


def kernel(
    n, ns, lesser, greater, diag_hbm, upper_hbm, out,
    diag, upper, gv, ht, held, lf, hf, cf, own_sum, own_low, cs, cin, late, polar, side, uprev, wside, total,
    local_sem, deal_send, deal_recv, z_send, z_recv, h_recv, c_send, c_recv, m_recv, late_recv, back_send, back_recv,
    side_send, side_recv, u_send, u_recv,
):
    me = lax.axis_index("energy")
    row = lax.axis_index("space")
    pieces, _, groups, block, _, _, _ = held.shape
    chunks, k, _, size, _ = polar.shape
    members = n // groups
    stack = members * TILE
    stacks = size // stack
    plane, member = me // members, lax.rem(me, members)
    has_next = row < ns - 1
    has_prev = row > 0
    straight_in = range(STRAIGHT_IN)
    straight_out = range(pieces - STRAIGHT_OUT, pieces)
    early = range(EARLY)
    merged = range(EARLY, pieces - STRAIGHT_OUT)

    def column(level):
        return to_energy(level * members + member)

    barrier = pltpu.get_barrier_semaphore()

    def greet(step, carry):
        peer = plane * members + lax.rem(member + step, members)
        pl.semaphore_signal(barrier, inc=1, device_id=to_energy(peer), device_id_type=MESH)
        return carry

    lax.fori_loop(1, members, greet, 0)

    @pl.when(plane == 0)
    def _():
        pl.semaphore_signal(barrier, inc=1, device_id=column(2), device_id_type=MESH)

    @pl.when(plane == 1)
    def _():
        pl.semaphore_signal(barrier, inc=1, device_id=column(0), device_id_type=MESH)

    @pl.when(plane == 2)
    def _():
        pl.semaphore_signal(barrier, inc=1, device_id=column(1), device_id_type=MESH)
        for peer in range(members):
            pl.semaphore_signal(barrier, inc=1, device_id=to_energy(3 * members + peer), device_id_type=MESH)

    @pl.when(has_next)
    def _():
        pl.semaphore_signal(barrier, inc=1, device_id=to_space(row + 1), device_id_type=MESH)

    @pl.when(has_prev)
    def _():
        pl.semaphore_signal(barrier, inc=1, device_id=to_space(row - 1), device_id_type=MESH)

    def load(c):
        rows = pl.ds(c * LANES, LANES)
        return pltpu.make_async_copy(greater.at[:, 0, :, rows, :], gv.at[:, :, rows, :], local_sem.at[c])

    for c in range(chunks):
        load(c).start()

    def turn_over(c):
        load(c).wait()
        cols = slice(c * LANES, (c + 1) * LANES)
        for e in range(k):
            for part_at in range(2):
                ht[e, part_at, :, cols] = gv[e, part_at, cols, :].T

    @pl.when(plane < 2)
    def _():
        turn_over(0)

    more_greet = (members - 1) * (plane == 3).astype(jnp.int32)
    pl.semaphore_wait(
        barrier, members + more_greet + has_next.astype(jnp.int32) + has_prev.astype(jnp.int32)
    )

    u_copy = pltpu.make_async_remote_copy(
        src_ref=upper_hbm.at[0], dst_ref=uprev, send_sem=u_send, recv_sem=u_recv,
        device_id=to_space(lax.rem(row + 1, ns)), device_id_type=MESH,
    )

    def tile_of(who):
        return pl.ds(pl.multiple_of(who * TILE, TILE), TILE)

    def share_rows(who, p):
        return pl.ds(pl.multiple_of((p % stacks) * stack + who * TILE, TILE), TILE)

    def piece_rows(p):
        return pl.ds((p % stacks) * stack, stack)

    def energies_of(who):
        return pl.ds(pl.multiple_of(who * k, k), k)

    def part(p, kind, who):
        source = (lesser.at[:, 0], ht)[kind]
        return source.at[:, :, share_rows(who, p), pl.ds((p // stacks) * LANES, LANES)]

    def deal(p, kind):
        landing = held.at[p, kind, plane, energies_of(member)]

        def push(step, carry):
            peer = lax.rem(member + step, members)
            pltpu.make_async_remote_copy(
                src_ref=part(p, kind, peer), dst_ref=landing,
                send_sem=deal_send.at[kind], recv_sem=deal_recv.at[kind, p],
                device_id=to_energy(plane * members + peer), device_id_type=MESH,
            ).start()
            return carry

        lax.fori_loop(1, members, push, 0)
        pltpu.make_async_copy(part(p, kind, member), landing, deal_recv.at[kind, p]).start()

    def drop(p, kind):
        def push(step, carry):
            peer = lax.rem(member + step, members)
            pltpu.make_async_remote_copy(
                src_ref=part(p, kind, peer), dst_ref=held.at[p, kind, 3, energies_of(member)],
                send_sem=z_send, recv_sem=z_recv.at[p],
                device_id=to_energy(2 * members + peer), device_id_type=MESH,
            ).start()
            return carry

        lax.fori_loop(0, members, push, 0)

    lead = min(AHEAD, pieces)

    @pl.when(plane < 2)
    def _():
        for p in range(lead):
            deal(p, 1)

    @pl.when(plane == 2)
    def _():
        deal(0, 0)
        turn_over(0)
        deal(0, 1)

    @pl.when(plane == 3)
    def _():
        drop(0, 0)
        turn_over(0)
        drop(0, 1)

    for c in range(1, chunks):
        turn_over(c)

    @pl.when(plane < 2)
    def _():
        for p in range(pieces):
            deal(p, 0)
            if p + lead < pieces:
                deal(p + lead, 1)

    @pl.when(plane == 2)
    def _():
        for p in range(1, pieces):
            deal(p, 0)
            deal(p, 1)

    @pl.when(plane == 3)
    def _():
        for p in range(1, pieces):
            for kind in range(2):
                if p in straight_in:
                    drop(p, kind)
                else:
                    deal(p, kind)

    load_upper = pltpu.make_async_copy(upper_hbm, upper, local_sem.at[chunks])
    load_upper.start()
    load_diag = pltpu.make_async_copy(diag_hbm, diag, local_sem.at[chunks + 1])
    load_diag.start()
    for both in range(2):
        lf[both] = jnp.zeros(lf.shape[1:], jnp.float32)

    @pl.when(has_next)
    def _():
        u_copy.start()

    def settle(ref, sem):
        pltpu.make_async_copy(ref, ref, sem).wait()

    def dealt(p, kind, level):
        settle(held.at[p, kind, level], deal_recv.at[kind, p])

    def lift(p, kind, level, to, recv):
        pltpu.make_async_remote_copy(
            src_ref=held.at[p, kind, level], dst_ref=held.at[p, kind, level], send_sem=z_send,
            recv_sem=recv.at[p], device_id=column(to), device_id_type=MESH,
        ).start()

    def give(p, lag_block, slot):
        pltpu.make_async_remote_copy(
            src_ref=cs.at[p, lag_block], dst_ref=cin.at[p, slot], send_sem=c_send,
            recv_sem=c_recv.at[p], device_id=column(lag_block), device_id_type=MESH,
        ).start()

    def give_home(p, lag_block):
        def push(step, carry):
            peer = lax.rem(member + step, members)
            pltpu.make_async_remote_copy(
                src_ref=cs.at[p, lag_block, energies_of(peer)],
                dst_ref=polar.at[p // stacks, :, :, share_rows(member, p), :],
                send_sem=c_send, recv_sem=back_recv.at[p],
                device_id=to_energy(lag_block * members + peer), device_id_type=MESH,
            ).start()
            return carry

        lax.fori_loop(0, members, push, 0)

    def give_straight(p, lag_block):
        at = p - straight_out[0]

        def push(step, carry):
            peer = lax.rem(member + step, members)
            pltpu.make_async_remote_copy(
                src_ref=cs.at[p, lag_block, energies_of(peer)], dst_ref=late.at[at, :, :, tile_of(member), :],
                send_sem=c_send, recv_sem=late_recv.at[at],
                device_id=to_energy(lag_block * members + peer), device_id_type=MESH,
            ).start()
            return carry

        lax.fori_loop(0, members, push, 0)

    def back(source, p):
        landing = polar.at[p // stacks, :, :, share_rows(member, p), :]

        def push(step, carry):
            peer = lax.rem(member + step, members)
            pltpu.make_async_remote_copy(
                src_ref=source.at[energies_of(peer)], dst_ref=landing,
                send_sem=back_send, recv_sem=back_recv.at[p],
                device_id=to_energy(plane * members + peer), device_id_type=MESH,
            ).start()
            return carry

        lax.fori_loop(1, members, push, 0)
        pltpu.make_async_copy(source.at[energies_of(member)], landing, back_recv.at[p]).start()

    def terms(source, coupler, c):
        right = coupler[:, c * LANES:(c + 1) * LANES]
        for e in range(k):
            pair = jnp.concatenate([source[e, 0], source[e, 1]], axis=1)
            left = jnp.dot(coupler, pair, preferred_element_type=jnp.float32).astype(jnp.bfloat16)
            for part_at in range(2):
                yield e, part_at, lax.dot_general(
                    left[:, part_at * LANES:(part_at + 1) * LANES], right,
                    (((1,), (1,)), ((), ())), preferred_element_type=jnp.float32,
                )

    def screen(source, coupler, c, begin):
        for e, part_at, term in terms(source, coupler, c):
            if begin:
                total[e, part_at] = term
            else:
                total[e, part_at] += term

    def finish(source, coupler, c):
        for e, part_at, term in terms(source, coupler, c):
            out[e, 0, part_at] = (total[e, part_at] + term).astype(jnp.bfloat16)

    up, down = lax.rem(row + 1, ns), lax.rem(row + ns - 1, ns)

    def forward(p, slot, to):
        place = (p // stacks, slice(None), slice(None), piece_rows(p))
        return pltpu.make_async_remote_copy(
            src_ref=polar.at[place], dst_ref=side.at[(slot,) + place], send_sem=side_send.at[slot],
            recv_sem=side_recv.at[slot, p // stacks], device_id=to_space(to), device_id_type=MESH,
        )

    def hand_over(p):
        place = (p // stacks, slice(None), slice(None), piece_rows(p))
        settle(polar.at[place], back_recv.at[p])
        if p in straight_out:
            @pl.when(plane < 2)
            def _():
                at = p - straight_out[0]
                settle(late.at[at], late_recv.at[at])
                both = polar[place].astype(jnp.float32) + late[at].astype(jnp.float32)
                polar[place] = both.astype(jnp.bfloat16)

        @pl.when(has_prev)
        def _():
            forward(p, 0, down).start()

        @pl.when(has_next)
        def _():
            forward(p, 1, up).start()

    def screen_own(c):
        for p in range(c * stacks, (c + 1) * stacks):
            hand_over(p)
        screen(polar.at[c], diag[0], c, c == 0)

    def from_next(c, act):
        @pl.when(has_next)
        def _():
            settle(side.at[0, c], side_recv.at[0, c])
            act(side.at[0, c], wside[0], c)

    def from_prev(c, act):
        @pl.when(has_prev)
        def _():
            settle(side.at[1, c], side_recv.at[1, c])
            act(side.at[1, c], wside[1], c)

    def more(source, coupler, c):
        screen(source, coupler, c, False)

    def screen_sides(c):
        from_next(c, more)
        from_prev(c, more)

    def couplers():
        load_upper.wait()
        load_diag.wait()
        wside[0] = upper[0]

        @pl.when(has_prev)
        def _():
            u_copy.wait_recv()
            wside[1] = uprev[...].T

    def add(p, lag_block, slots):
        value = own_sum[p]
        if slots:
            settle(cin.at[p, pl.ds(0, slots)], c_recv.at[p])
        for slot in range(slots):
            value = value + cin[p, slot].astype(jnp.float32)
        cs[p, lag_block] = value.astype(jnp.bfloat16)
        back(cs.at[p, lag_block], p)

    def rounded(p, lag_block):
        cs[p, lag_block] = cf[...].astype(jnp.bfloat16)

    def give_middle(p):
        pltpu.make_async_remote_copy(
            src_ref=cs.at[p, 0], dst_ref=cin.at[p, 1], send_sem=c_send,
            recv_sem=m_recv.at[p], device_id=column(1), device_id_type=MESH,
        ).start()

    def merge(p):
        settle(cin.at[p, 1], m_recv.at[p])
        cs[p, 0] = (own_low[p] + cin[p, 1].astype(jnp.float32)).astype(jnp.bfloat16)
        give(p, 0, 0)

    @pl.when(plane == 0)
    def _():
        def send(p):
            dealt(p, 1, 0)
            lift(p, 1, 0, 1, h_recv)

        for p in range(pieces):
            send(p)
        for p in range(pieces):
            dealt(p, 0, 0)
            widen_into(lf.at[0], 0, held[p, 0, 0])
            widen_into(hf.at[0], 0, held[p, 1, 0])
            correlate_into(own_sum.at[p], lf.at[0], hf.at[0], 0, block, 0, 1)
        for p in (*early, *straight_out, *merged):
            add(p, 0, 2 if p in early else 1)

    @pl.when(plane == 1)
    def _():
        def send(p):
            dealt(p, 1, 1)
            lift(p, 1, 1, 2, z_recv)

        for p in range(FIRST):
            send(p)
        for p in range(pieces):
            settle(held.at[p, 1, 0], h_recv.at[p])
            lift(p, 1, 0, 2, h_recv)
            if p + FIRST < pieces:
                send(p + FIRST)
            dealt(p, 0, 1)
            widen_into(lf.at[0], 1, held[p, 0, 1])
            widen_into(hf.at[0], 1, held[p, 1, 1])
            widen_into(hf.at[0], 0, held[p, 1, 0])
            if p in merged:
                correlate_into(own_low.at[p], lf.at[0], hf.at[0], 0, block, 1, 2)
            else:
                correlate_into(cf, lf.at[0], hf.at[0], 0, block, 1, 2)
                rounded(p, 0)
                give(p, 0, 0)
            correlate_into(own_sum.at[p], lf.at[0], hf.at[0], 1, block, 1, 2)
        for p in straight_out:
            add(p, 1, 0)
        for p in (*early, *merged):
            if p + 1 in merged:
                merge(p + 1)
            add(p, 1, 1)

    @pl.when(plane == 2)
    def _():
        def share(p, lag_block):
            if p in straight_out:
                give_straight(p, lag_block)
            elif p in merged and lag_block == 0:
                give_middle(p)
            else:
                give(p, lag_block, 1 - lag_block)

        def lags(p, lag_block):
            correlate_into(cf, lf.at[p % 2], hf.at[p % 2], lag_block, block, 2, groups)
            rounded(p, lag_block)

        def lowest(p):
            wide_l, wide_h = lf.at[p % 2], hf.at[p % 2]
            dealt(p, 0, 2)
            dealt(p, 1, 2)
            widen_into(wide_l, 2, held[p, 0, 2])
            widen_into(wide_h, 2, held[p, 1, 2])
            settle(held.at[p, 0, pl.ds(0, 3)], z_recv.at[p])
            widen_into(wide_l, 3, held[p, 0, 3])
            widen_into(wide_h, 3, held[p, 1, 3])
            widen_into(wide_h, 1, held[p, 1, 1])
            lags(p, 0)
            share(p, 0)

        def next_lowest(p):
            settle(held.at[p, 1, 0], h_recv.at[p])
            widen_into(hf.at[p % 2], 0, held[p, 1, 0])
            lags(p, 1)
            share(p, 1)

        def highest(p):
            lags(p, 3)
            give_home(p, 3)

        def own_lags(p):
            lags(p, 2)
            back(cs.at[p, 2], p)

        for p in range(pieces - 1):
            lowest(p)
            if p:
                for act in (next_lowest, highest, own_lags):
                    act(p - 1)
        lowest(pieces - 1)
        for act in (next_lowest, highest, own_lags):
            act(pieces - 2)
            act(pieces - 1)

    @pl.when(plane == 3)
    def _():
        for p in range(pieces):
            if p not in straight_in:
                for kind in range(2):
                    dealt(p, kind, 3)
                    lift(p, kind, 3, 2, z_recv)

    couplers()
    for c in range(chunks - 1):
        screen_own(c)
    for c in range(chunks - 1):
        screen_sides(c)
    last = chunks - 1
    screen_own(last)

    @pl.when(jnp.logical_and(has_prev, has_next))
    def _():
        from_next(last, more)

    @pl.when(has_prev)
    def _():
        settle(side.at[1, last], side_recv.at[1, last])
        finish(side.at[1, last], wside[1], last)

    @pl.when(row == 0)
    def _():
        settle(side.at[0, last], side_recv.at[0, last])
        finish(side.at[0, last], wside[0], last)

    @pl.when(has_prev)
    def _():
        settle(polar, side_send.at[0])

    @pl.when(has_next)
    def _():
        settle(polar, side_send.at[1])
        u_copy.wait_send()

    others = pl.ds(0, k * (members - 1))

    @pl.when(plane < 3)
    def _():
        settle(held.at[:, 0, 0, others], back_send)
        for kind in range(2):
            settle(held.at[:, kind, 0, others], deal_send.at[kind])

    @pl.when(plane == 0)
    def _():
        settle(held.at[:, 0, 0], z_send)

    @pl.when(plane == 1)
    def _():
        settle(held.at[:, 0, pl.ds(0, 2)], z_send)
        settle(cs.at[:, 0], c_send)

    @pl.when(plane == 2)
    def _():
        settle(cs.at[:, pl.ds(0, 3)], c_send)

    @pl.when(plane == 3)
    def _():
        settle(held.at[:, 0, pl.ds(0, 2)], z_send)
        for kind in range(2):
            settle(held.at[pl.ds(0, pieces - STRAIGHT_IN), kind, 0, others], deal_send.at[kind])


def fused(n, ns, lesser, greater, diag, upper):
    k, _, _, size, _ = lesser.shape
    members, energies, chunks = n // GROUPS, n * k, size // LANES
    block = members * k
    pieces = chunks * (size // members // TILE)
    bf, f32 = jnp.bfloat16, jnp.float32
    whole = (k, 2, size, size)
    piece = (block, 2, TILE, LANES)
    padded = energies + LAGS + STEPS
    dma = pltpu.SemaphoreType.DMA
    vmem = pl.BlockSpec(memory_space=pltpu.VMEM)
    hbm = pl.BlockSpec(memory_space=pltpu.HBM)
    return pl.pallas_call(
        functools.partial(kernel, n, ns),
        out_shape=jax.ShapeDtypeStruct(lesser.shape, bf),
        in_specs=[hbm] * 4,
        out_specs=vmem,
        scratch_shapes=[
            pltpu.VMEM(diag.shape, bf),
            pltpu.VMEM(upper.shape, bf),
            pltpu.VMEM(whole, bf),
            pltpu.VMEM(whole, bf),
            pltpu.VMEM((pieces, 2, GROUPS) + piece, bf),
            pltpu.VMEM((2, 3, padded, TILE, LANES), f32),
            pltpu.VMEM((2, 3, energies, TILE, LANES), f32),
            pltpu.VMEM(piece, f32),
            pltpu.VMEM((pieces,) + piece, f32),
            pltpu.VMEM((pieces,) + piece, f32),
            pltpu.VMEM((pieces, GROUPS) + piece, bf),
            pltpu.VMEM((pieces, 2) + piece, bf),
            pltpu.VMEM((STRAIGHT_OUT, k, 2, members * TILE, LANES), bf),
            pltpu.VMEM((chunks, k, 2, size, LANES), bf),
            pltpu.VMEM((2, chunks, k, 2, size, LANES), bf),
            pltpu.VMEM((size, size), bf),
            pltpu.VMEM((2, size, size), bf),
            pltpu.VMEM(whole, f32),
            dma((chunks + 2,)), dma((2,)), dma((2, pieces)), dma, dma((pieces,)), dma((pieces,)), dma,
            dma((pieces,)), dma((pieces,)), dma((STRAIGHT_OUT,)), dma, dma((pieces,)), dma((2,)), dma((2, chunks)), dma, dma,
        ],
        compiler_params=pltpu.CompilerParams(
            collective_id=0, has_side_effects=True, vmem_limit_bytes=40 << 20
        ),
    )(*(pltpu.with_memory_space_constraint(x, pltpu.HBM) for x in (lesser, greater, diag, upper)))


def fits(n, ns, size, k):
    if n % GROUPS or size % LANES or size <= LANES or ns < 2:
        return False
    members = n // GROUPS
    if members < 2 or size % (members * TILE) or (members * k) % STEPS:
        return False
    stacks = size // members // TILE
    return 2 <= stacks and EARLY + STRAIGHT_OUT < size // LANES * stacks <= 16


def either(n, ns, lesser, greater, diag, upper):
    if fits(n, ns, lesser.shape[3], lesser.shape[0]):
        return fused(n, ns, lesser, greater, diag, upper)
    return per_device(lesser, greater, diag, upper)


def solution(mesh):
    placed = (
        P("energy", "space", None, None, None),
        P("energy", "space", None, None, None),
        P("space", None, None),
        P("space", None, None),
    )
    return jax.shard_map(
        functools.partial(either, mesh.shape["energy"], mesh.shape["space"]),
        mesh=mesh,
        in_specs=placed,
        out_specs=P("energy", "space", None, None, None),
        check_vma=False,
    )
```
